256 devices in a mesh: rcv: 4 (over y_lo, core), slab: 64 (over z, y_hi, x).
Axes of the slice: x: 4, y: 4 (y_hi: 2, y_lo: 2; y = y_hi * 2 + y_lo), z: 8, core: 2. Of those that a mesh axis runs over, the one named last changes fastest.
Arguments:
- displacement: bfloat16 [2, 16, 3, 128, 16, 1024], P(None, None, None, 'slab'), may hold values from -6 to 6
- green: bfloat16 [8, 16, 6, 128, 16, 1024], P('rcv', None, None, 'slab'), may hold values from -0.1796875 to 0.1796875
- lame_lambda: float32 [128, 16, 1024], P('slab'), may hold values from 0.5 to 2
- shear_modulus: float32 [128, 16, 1024], P('slab'), may hold values from 0.3 to 1.5
- filters: float32 [2, 8, 9], P(None, 'rcv'), may hold values from -2 to 2
- pairs: int32 [2, 8], P(None, 'rcv'), may hold values 0 or 1
Outputs:
- kernels: float32 [2, 128, 16, 1024], P(None, 'slab', 'rcv')
The draws below stay inside these ranges and needn't reach their ends.
Inputs may be any that keep to these rules, and one draw needn't show every extreme that they name: `pairs`: 1 marks a pair that is used, 0 one that is not.
All inputs are finite; a program needn't handle non-finite values. No bound on the sum of `pairs` on one device may be relied on, other than what follows from the above.
Results may differ from the reference program's by a relative error of at most 0.0029.
Values may be sent and summed in bfloat16 or wider, within the bound.
A program may use at most 192 MiB of HBM per device.

```python
import math
import jax
import jax.numpy as jnp
from jax import lax

E = 2
SNAP = 16
LAGS = 9
ROWS = 16
COLS = 1024
NZ = 128
RECEIVERS = 8


def with_ends(values, rng, least, high):
    shape = values.shape
    spot = [jax.random.randint(jax.random.fold_in(rng, axis), (), 0, shape[axis]) for axis in range(len(shape))]
    values = values.at[tuple(spot)].set(least)
    longest = shape.index(max(shape))
    spot[longest] = (spot[longest] + 1) % shape[longest]
    return values.at[tuple(spot)].set(high)


def raised(values, own_key, source, target, shards_of, factor):
    def block_of(axis_at):
        return (jnp.arange(values.shape[axis_at]) // (values.shape[axis_at] // shards_of)).reshape((-1,) + (1,) * (values.ndim - 1 - axis_at))

    first = jax.random.permutation(own_key, shards_of)[block_of(target)]
    second = (block_of(target) + shards_of // 2) % shards_of
    return jnp.where((block_of(source) == first) | (block_of(source) == second), factor * values, values)


def steps_of(rng, shape, pieces, smallest, top_value):
    loudness, own = 1.0, jax.random.fold_in(rng, 6)
    for dim, blocks in pieces:
        heights = jnp.exp(jax.random.uniform(jax.random.fold_in(own, dim), (blocks,), jnp.float32, smallest / len(pieces), top_value / len(pieces)))
        loudness = loudness * jnp.repeat(heights, shape[dim] // blocks).reshape([-1 if axis == dim else 1 for axis in range(len(shape))])
    return loudness


def scatter_about(key, dims, deviation, most, split=(), dtype=jnp.bfloat16):
    entries = deviation * jax.random.normal(key, dims, jnp.float32)
    if split:
        entries = entries * steps_of(key, dims, split, -0.22, 0.18)
    return jnp.clip(entries, -most, most).astype(dtype)


def heavy_noise(key, dims, scale, limit, cuts, heavy, dtype=jnp.bfloat16):
    values = scale * jax.random.normal(key, dims, jnp.float32)
    if cuts:
        values = values * steps_of(key, dims, cuts, -0.22, 0.18)
    return jnp.clip(raised(values, jax.random.fold_in(key, 3), *heavy), -limit, limit).astype(dtype)


def setup_inputs(seed: int = 0) -> dict:
    key_of = jax.random.split(jax.random.key(seed), 7)
    return {
        "displacement": scatter_about(key_of[0], (E, SNAP, 3, NZ, ROWS, COLS), 1.0, 6.0, ((3, 64),)),
        "green": heavy_noise(key_of[1], (RECEIVERS, SNAP, 6, NZ, ROWS, COLS), 0.03, 0.1796875, ((0, 4), (3, 64)), (0, 4, 4, 2.0)),
        "lame_lambda": jnp.clip(jnp.exp(math.log(2.0) - 1.3862944 * jax.random.uniform(key_of[2], (NZ, ROWS, COLS), jnp.float32) ** steps_of(key_of[2], (NZ, ROWS, COLS), ((0, 64),), -0.2, 0.2)), 0.5, 2.0),
        "shear_modulus": jnp.clip(jnp.exp(math.log(1.5) - 1.60943787 * jax.random.uniform(key_of[3], (NZ, ROWS, COLS), jnp.float32) ** steps_of(key_of[3], (NZ, ROWS, COLS), ((0, 64),), -0.2, 0.2)), 0.3, 1.5),
        "filters": scatter_about(key_of[4], (E, RECEIVERS, LAGS), 0.35, 2.0, ((1, 4),), jnp.float32),
        "pairs": with_ends((jax.random.randint(key_of[5], (E, RECEIVERS), 0, 2) < 1).astype(jnp.int32), jax.random.fold_in(key_of[5], 1), 0, 1),
    }


def derivative(field, axis):
    length = field.shape[axis]
    pad_width = [(0, 0)] * field.ndim
    pad_width[axis] = (2, 2)
    padded = jnp.pad(field, pad_width)

    def window(offset):
        return lax.slice_in_dim(padded, 2 + offset, 2 + offset + length, axis=axis)

    return (8.0 * (window(1) - window(-1)) - (window(2) - window(-2))) / 12.0


def compose(along_cols, along_rows, along_depth, lame_lambda, shear_modulus):
    strain_xx = along_cols[:, :, 0]
    strain_yy = along_rows[:, :, 1]
    strain_zz = along_depth[:, :, 2]
    strain_yz = 0.5 * (along_depth[:, :, 1] + along_rows[:, :, 2])
    strain_xz = 0.5 * (along_depth[:, :, 0] + along_cols[:, :, 2])
    strain_xy = 0.5 * (along_rows[:, :, 0] + along_cols[:, :, 1])
    strain_trace = strain_xx + strain_yy + strain_zz
    volume_term = lame_lambda * strain_trace
    double_shear = 2.0 * shear_modulus
    components = [volume_term + double_shear * strain_xx, volume_term + double_shear * strain_yy,
                  volume_term + double_shear * strain_zz, double_shear * strain_yz,
                  double_shear * strain_xz, double_shear * strain_xy]
    return jnp.stack(components, axis=2).astype(jnp.bfloat16)


def contribution(stress_one, filter_taps, green_one):
    lag_total = filter_taps.shape[0]
    half_lags = lag_total // 2
    snap_count = stress_one.shape[0]
    padded = jnp.pad(stress_one, [(half_lags, half_lags)] + [(0, 0)] * (stress_one.ndim - 1))
    filtered = jnp.zeros(stress_one.shape, jnp.float32)
    for lag_index in range(lag_total):
        filtered = filtered + filter_taps[lag_index] * padded[lag_index:lag_index + snap_count].astype(jnp.float32)
    weights = jnp.array([1.0, 1.0, 1.0, 2.0, 2.0, 2.0], jnp.float32).reshape(1, 6, 1, 1, 1)
    return jnp.sum(filtered * green_one.astype(jnp.float32) * weights, axis=(0, 1))


def reference(displacement, green, lame_lambda, shear_modulus, filters, pairs):
    field = displacement.astype(jnp.float32)
    along_cols = derivative(field, 5)
    along_rows = derivative(field, 4)
    along_depth = derivative(field, 3)
    stress = compose(along_cols, along_rows, along_depth, lame_lambda, shear_modulus)
    initial = jnp.zeros((E, NZ, ROWS, COLS), jnp.float32)

    def receiver_step(kernel_total, scanned):
        green_one, filter_rows, pair_row = scanned
        per_source = [pair_row[source].astype(jnp.float32) * contribution(stress[source], filter_rows[source], green_one)
                      for source in range(E)]
        return kernel_total + jnp.stack(per_source), None

    kernel_total, unused = lax.scan(receiver_step, initial,
                                    (green, jnp.swapaxes(filters, 0, 1), jnp.swapaxes(pairs, 0, 1)))
    return kernel_total
```

```python
import functools

import jax
import jax.numpy as jnp
from jax import lax
from jax.experimental import pallas as pl
from jax.experimental.pallas import tpu as pltpu
from jax.sharding import PartitionSpec as P

MESH = pl.DeviceIdType.MESH
F32, BF16 = jnp.float32, jnp.bfloat16
ROW = 16
LANES = 128
WIDE = 256
RING_X = 4
WINDOW = 2


def iota2(shape, axis):
    return lax.broadcasted_iota(jnp.int32, shape, axis)


def stencil(offset):
    eight = jnp.where(offset == 1, 8.0, jnp.where(offset == -1, -8.0, 0.0))
    return jnp.where(offset == 2, -1.0, jnp.where(offset == -2, 1.0, eight))


def kernel(
    sources, snaps, stations, lags,
    u_hbm, g_hbm, lam_hbm, mu_hbm, filt, pairs, out_ref,
    uv, gv, lamv, muv, halo, dz, adj, hbuf, dxb, dyb, mix_hi, mix_lo, colmat, rowmat, kacc, kpart, red,
    u_sem, g_sem, lam_sem, mu_sem,
    halo_send, halo_recv, sib_send, sib_recv, par_send, par_recv, fwd_send, fwd_recv, red_send, red_recv,
):
    slots = sources * snaps
    quarter = slots // 4
    pieces = dz.shape[0]
    blocks = gv.shape[0]
    cols = u_hbm.shape[-1]

    rcv, slab = lax.axis_index("rcv"), lax.axis_index("slab")
    slabs = lax.axis_size("slab")
    sibling = rcv + 1 - 2 * (rcv % 2)
    partner = (rcv + 2) % 4
    diagonal = (sibling + 2) % 4
    up_rcv = (rcv + 2 * ((slab % RING_X + 1) // RING_X)) % 4
    down_rcv = (rcv + 2 * ((RING_X - slab % RING_X) // RING_X)) % 4
    up = {"slab": (slab + 1) % slabs, "rcv": up_rcv}
    down = {"slab": (slab + slabs - 1) % slabs, "rcv": down_rcv}
    has_below = ((slab + slabs - 1) // slabs).astype(F32)
    has_above = ((2 * slabs - 2 - slab) // slabs).astype(F32)

    u_copy = pltpu.make_async_copy(u_hbm, uv.at[:, :, :, :, pl.ds(LANES, cols)], u_sem)
    u_copy.start()

    def g_copy(block):
        return pltpu.make_async_copy(
            g_hbm.at[:, :, :, :, pl.ds(pl.multiple_of(block * WIDE, WIDE), WIDE)], gv.at[block], g_sem.at[block])

    for block in range(blocks):
        g_copy(block).start()
    lam_copy = pltpu.make_async_copy(lam_hbm, lamv, lam_sem)
    mu_copy = pltpu.make_async_copy(mu_hbm, muv, mu_sem)
    lam_copy.start()
    mu_copy.start()

    barrier = pltpu.get_barrier_semaphore()
    peers = (up, down, {"rcv": sibling}, {"rcv": partner}, {"rcv": diagonal})
    for peer in peers:
        pl.semaphore_signal(barrier, inc=1, device_id=peer, device_id_type=MESH)
    pl.semaphore_wait(barrier, len(peers))

    def halo_copy(side, piece):
        target, their = ((up, up_rcv), (down, down_rcv))[side]
        return pltpu.make_async_remote_copy(
            src_ref=u_hbm.at[pl.ds(their * quarter, quarter), :, :, :, pl.ds(pl.multiple_of(piece * LANES, LANES), LANES)],
            dst_ref=halo.at[side, piece],
            send_sem=halo_send.at[side, piece], recv_sem=halo_recv.at[side, piece],
            device_id=target, device_id_type=MESH)

    def share_copy(piece, of, target, send, recv):
        block = dz.at[piece, pl.ds(of * quarter, quarter)]
        return pltpu.make_async_remote_copy(
            src_ref=block, dst_ref=block, send_sem=send.at[piece], recv_sem=recv.at[piece],
            device_id={"rcv": target}, device_id_type=MESH)

    def to_sibling(piece):
        return share_copy(piece, rcv, sibling, sib_send, sib_recv)

    def to_partner(piece):
        return share_copy(piece, rcv, partner, par_send, par_recv)

    def forward(piece):
        return share_copy(piece, partner, sibling, fwd_send, fwd_recv)

    def red_copy(which, piece):
        target = (sibling, partner, diagonal)[which]
        return pltpu.make_async_remote_copy(
            src_ref=kpart.at[piece, target], dst_ref=red.at[which, piece],
            send_sem=red_send.at[which, piece], recv_sem=red_recv.at[which, piece],
            device_id={"rcv": target}, device_id_type=MESH)

    for piece in range(WINDOW):
        for side in range(2):
            halo_copy(side, piece).start()

    a, b = iota2((slots, stations * snaps), 0), iota2((slots, stations * snaps), 1)
    lag = a % snaps - b % snaps + lags // 2
    taps = jnp.zeros((slots, stations * snaps), F32)
    for source in range(sources):
        for station in range(stations):
            used = pairs[source, station].astype(F32)
            here = (a // snaps == source) & (b // snaps == station)
            for j in range(lags):
                taps = taps + jnp.where(here & (lag == j), filt[source, station, j] * used, 0.0)
    high = taps.astype(BF16)
    low = (taps - high.astype(F32)).astype(BF16)
    size = slots * ROW
    spread = (iota2((size, slots), 0) // ROW == iota2((size, slots), 1)).astype(BF16)
    depth = stations * snaps * ROW
    spread_t = (iota2((stations * snaps, depth), 0) == iota2((stations * snaps, depth), 1) // ROW).astype(BF16)
    same_row = iota2((size, depth), 0) % ROW == iota2((size, depth), 1) % ROW
    for part, target in ((high, mix_hi), (low, mix_lo)):
        tall = jnp.dot(spread, part, preferred_element_type=F32).astype(BF16)
        target[...] = jnp.where(same_row, jnp.dot(tall, spread_t, preferred_element_type=F32), 0.0).astype(BF16)
    i, o = iota2(colmat.shape, 0), iota2(colmat.shape, 1)
    colmat[...] = stencil(i - LANES - o).astype(BF16)
    i, o = iota2(rowmat.shape, 1), iota2(rowmat.shape, 0)
    rowmat[...] = jnp.where(i // ROW == o // ROW, stencil(i - o), 0.0).astype(BF16)
    edge = jnp.zeros(uv.shape[:-1] + (LANES,), BF16)
    u_copy.wait()
    uv[:, :, :, :, :LANES] = edge
    uv[:, :, :, :, LANES + cols:] = edge
    lam_copy.wait()
    mu_copy.wait()

    half = slots // 2

    def early(step):
        block, plane = step // 2, step % 2
        slot = block % 2

        @pl.when(plane == 0)
        def _():
            g_copy(block).wait()

        def mix(c, _):
            g = gv[block, :, c, plane].reshape(depth, WIDE)
            hbuf[c] = (jnp.dot(mix_hi[...], g, preferred_element_type=F32)
                       + jnp.dot(mix_lo[...], g, preferred_element_type=F32))
            return 0

        lax.fori_loop(0, 6, mix, 0)
        start = pl.multiple_of(block * WIDE, WIDE)

        def derive(k, _):
            around = uv[:, k, plane, :, pl.ds(start, 2 * WIDE)].reshape(size, 2 * WIDE)
            dxb[k] = jnp.dot(around, colmat[...], preferred_element_type=F32)
            inside = pl.ds(pl.multiple_of(start + LANES, LANES), WIDE)
            for part in range(2):
                rows = uv[part * half:(part + 1) * half, k, plane, :, inside].reshape(half * ROW, WIDE)
                dyb[k, part * half * ROW:(part + 1) * half * ROW] = jnp.dot(
                    rowmat[...], rows, preferred_element_type=F32)
            return 0

        lax.fori_loop(0, 3, derive, 0)
        lam = lamv[plane, :, pl.ds(start, WIDE)]
        shear = 2.0 * muv[plane, :, pl.ds(start, WIDE)]

        for source in range(sources):
            def weigh(t, carry):
                trace, rest = carry
                at = source * snaps + t
                here = pl.ds(pl.multiple_of(at * ROW, ROW), ROW)
                h = [hbuf[c, here] for c in range(6)]
                dx = [dxb[k, here] for k in range(3)]
                dy = [dyb[k, here] for k in range(3)]
                total = h[0] + h[1] + h[2]
                trace = trace + (dx[0] + dy[1]) * total
                rest = rest + (dx[0] * h[0] + dy[1] * h[1] + dy[2] * h[3] + dx[2] * h[4] + (dy[0] + dx[1]) * h[5])
                for k, value in enumerate((shear * h[4], shear * h[3], lam * total + shear * h[2])):
                    for side in range(2):
                        adj[slot, side, k, at, plane] = value[:, side * LANES:(side + 1) * LANES]
                return trace, rest

            zero = jnp.zeros((ROW, WIDE), F32)
            trace, rest = lax.fori_loop(0, snaps, weigh, (zero, zero))
            value = lam * trace + shear * rest
            for side in range(2):
                kacc[2 * block + side, source, plane] = value[:, side * LANES:(side + 1) * LANES]

    def depth_derivative(piece):
        here = pl.ds(pl.multiple_of(LANES + piece * LANES, LANES), LANES)

        def one(n, _):
            at = rcv * quarter + n
            for k in range(3):
                f0, f1 = (uv[at, k, plane, :, here].astype(F32) for plane in range(2))
                b0, b1 = (has_below * halo[0, piece, n, k, plane].astype(F32) for plane in range(2))
                a0, a1 = (has_above * halo[1, piece, n, k, plane].astype(F32) for plane in range(2))
                dz[piece, at, k, 0] = (8.0 * (f1 - b1) - (a0 - b0)).astype(BF16)
                dz[piece, at, k, 1] = (8.0 * (a0 - f0) - (a1 - b1)).astype(BF16)
            return 0

        lax.fori_loop(0, quarter, one, 0)

    def late(piece):
        slot, side = (piece // 2) % 2, piece % 2
        for source in range(sources):
            def add(t, totals):
                at = source * snaps + t
                new = []
                for plane in range(2):
                    total = totals[plane]
                    for k in range(3):
                        total = total + dz[piece, at, k, plane].astype(F32) * adj[slot, side, k, at, plane]
                    new.append(total)
                return tuple(new)

            totals = lax.fori_loop(0, snaps, add, tuple(kacc[piece, source, plane] for plane in range(2)))
            for plane in range(2):
                value = totals[plane] * (1.0 / 12.0)
                for owner in range(4):
                    kpart[piece, owner, source, plane] = value[owner * (ROW // 4):(owner + 1) * (ROW // 4)]

    def step(s, _):
        @pl.when(s < pieces)
        def _():
            early(s)
            for side in range(2):
                halo_copy(side, s).wait()
            @pl.when(s + WINDOW < pieces)
            def _():
                for side in range(2):
                    halo_copy(side, s + WINDOW).start()
            depth_derivative(s)
            to_partner(s).start()
            to_sibling(s).start()

        @pl.when((s >= 1) & (s <= pieces))
        def _():
            to_partner(s - 1).wait()
            forward(s - 1).start()

        @pl.when(s >= 2)
        def _():
            to_sibling(s - 2).wait()
            forward(s - 2).wait()
            late(s - 2)
            for which in range(3):
                red_copy(which, s - 2).start()
        return 0

    lax.fori_loop(0, pieces + 2, step, 0)

    for piece in range(pieces):
        for which in range(3):
            red_copy(which, piece).wait()
        out_ref[:, :, :, piece * LANES:(piece + 1) * LANES] = (
            (kpart[piece, rcv] + red[0, piece]) + (red[1, piece] + red[2, piece]))


def on_device(displacement, green, lame_lambda, shear_modulus, filters, pairs):
    sources, snaps, parts, planes, rows, cols = displacement.shape
    stations, lags = filters.shape[1:]
    slots, taps = sources * snaps, stations * snaps
    pieces, blocks, quarter = cols // LANES, cols // WIDE, slots // 4
    size, depth = slots * ROW, taps * ROW
    anywhere = pl.BlockSpec(memory_space=pl.ANY)
    scalars = pl.BlockSpec(memory_space=pltpu.SMEM)
    dma = pltpu.SemaphoreType.DMA
    return pl.pallas_call(
        functools.partial(kernel, sources, snaps, stations, lags),
        out_shape=jax.ShapeDtypeStruct((sources, planes, rows // 4, cols), F32),
        in_specs=[anywhere] * 4 + [scalars] * 2,
        out_specs=pl.BlockSpec(memory_space=pltpu.VMEM),
        scratch_shapes=[
            pltpu.VMEM((slots, parts, planes, rows, cols + 2 * LANES), BF16),
            pltpu.VMEM((blocks, taps, 6, planes, rows, WIDE), BF16),
            pltpu.VMEM((planes, rows, cols), F32),
            pltpu.VMEM((planes, rows, cols), F32),
            pltpu.VMEM((2, pieces, quarter, parts, planes, rows, LANES), BF16),
            pltpu.VMEM((pieces, slots, parts, planes, rows, LANES), BF16),
            pltpu.VMEM((2, 2, parts, slots, planes, rows, LANES), F32),
            pltpu.VMEM((6, size, WIDE), F32),
            pltpu.VMEM((3, size, WIDE), F32),
            pltpu.VMEM((3, size, WIDE), F32),
            pltpu.VMEM((size, depth), BF16),
            pltpu.VMEM((size, depth), BF16),
            pltpu.VMEM((2 * WIDE, WIDE), BF16),
            pltpu.VMEM((size // 2, size // 2), BF16),
            pltpu.VMEM((pieces, sources, planes, rows, LANES), F32),
            pltpu.VMEM((pieces, 4, sources, planes, rows // 4, LANES), F32),
            pltpu.VMEM((3, pieces, sources, planes, rows // 4, LANES), F32),
            dma, dma((blocks,)), dma, dma,
            dma((2, pieces)), dma((2, pieces)),
            dma((pieces,)), dma((pieces,)), dma((pieces,)), dma((pieces,)), dma((pieces,)), dma((pieces,)),
            dma((3, pieces)), dma((3, pieces)),
        ],
        compiler_params=pltpu.CompilerParams(
            collective_id=0, has_side_effects=True, vmem_limit_bytes=60 << 20),
        cost_estimate=pl.CostEstimate(flops=26_000_000_000, bytes_accessed=20_000_000, transcendentals=0),
    )(
        displacement.reshape(slots, parts, planes, rows, cols),
        green.reshape(taps, 6, planes, rows, cols),
        lame_lambda, shear_modulus, filters, pairs,
    )


def solution(mesh):
    placed = (
        P(None, None, None, "slab", None, None),
        P("rcv", None, None, "slab", None, None),
        P("slab", None, None),
        P("slab", None, None),
        P(None, "rcv", None),
        P(None, "rcv"),
    )
    return jax.shard_map(
        on_device,
        mesh=mesh,
        in_specs=placed,
        out_specs=P(None, "slab", "rcv", None),
        check_vma=False,
    )
```

```python
import functools

import jax
import jax.numpy as jnp
from jax import lax
from jax.experimental import pallas as pl
from jax.experimental.pallas import tpu as pltpu
from jax.sharding import PartitionSpec as P

MESH = pl.DeviceIdType.MESH
F32, BF16 = jnp.float32, jnp.bfloat16
ROW = 16
LANES = 128
WIDE = 256
RING_X = 4
HALF = ROW // 2
CUTS = 2


def iota2(shape, axis):
    return lax.broadcasted_iota(jnp.int32, shape, axis)


def stencil(offset):
    eight = jnp.where(offset == 1, 8.0, jnp.where(offset == -1, -8.0, 0.0))
    return jnp.where(offset == 2, -1.0, jnp.where(offset == -2, 1.0, eight))


def kernel(
    sources, snaps, stations, lags,
    u_hbm, g_hbm, lam_hbm, mu_hbm, filt, pairs, out_ref,
    uv, gv, lamv, muv, halo, dz, adj, hbuf, dxb, dyb, mixer, colmat, rowmat, kacc, kpart, red,
    u_sem, g_sem, lam_sem, mu_sem,
    halo_send, halo_recv, sib_send, sib_recv, par_send, par_recv, fwd_send, fwd_recv, red_send, red_recv,
):
    slots = sources * snaps
    quarter = slots // 4
    cut = quarter // CUTS
    pieces = dz.shape[0]
    blocks = gv.shape[0]
    cols = u_hbm.shape[-1]

    rcv, slab = lax.axis_index("rcv"), lax.axis_index("slab")
    slabs = lax.axis_size("slab")
    sibling = rcv + 1 - 2 * (rcv % 2)
    partner = (rcv + 2) % 4
    diagonal = (sibling + 2) % 4
    up_rcv = (rcv + 2 * ((slab % RING_X + 1) // RING_X)) % 4
    down_rcv = (rcv + 2 * ((RING_X - slab % RING_X) // RING_X)) % 4
    up = {"slab": (slab + 1) % slabs, "rcv": up_rcv}
    down = {"slab": (slab + slabs - 1) % slabs, "rcv": down_rcv}
    has_above, has_below = slab < slabs - 1, slab > 0
    count_above, count_below = (2 * slabs - 2 - slab) // slabs, (slabs - 1 + slab) // slabs

    u_copy = pltpu.make_async_copy(u_hbm, uv.at[:, :, :, :, pl.ds(LANES, cols)], u_sem)

    def g_copy(block):
        return pltpu.make_async_copy(
            g_hbm.at[:, :, :, :, pl.ds(pl.multiple_of(block * WIDE, WIDE), WIDE)], gv.at[block], g_sem.at[block])

    g_copy(0).start()
    u_copy.start()
    for block in range(1, blocks):
        g_copy(block).start()
    lam_copy = pltpu.make_async_copy(lam_hbm, lamv, lam_sem)
    mu_copy = pltpu.make_async_copy(mu_hbm, muv, mu_sem)
    lam_copy.start()
    mu_copy.start()

    barrier = pltpu.get_barrier_semaphore()
    def greet(peer):
        pl.semaphore_signal(barrier, inc=1, device_id=peer, device_id_type=MESH)

    def at_sides(condition_up, condition_down, act):
        for side, condition in enumerate((condition_up, condition_down)):
            @pl.when(condition)
            def _(side=side):
                act(side)

    at_sides(has_above, has_below, lambda side: greet((up, down)[side]))
    for peer in (sibling, partner, diagonal):
        greet({"rcv": peer})
    pl.semaphore_wait(barrier, 3 + count_above + count_below)

    def halo_copy(side, piece, part):
        target, their = ((up, up_rcv), (down, down_rcv))[side]
        return pltpu.make_async_remote_copy(
            src_ref=u_hbm.at[pl.ds(their * quarter + part * cut, cut), :, :, :,
                             pl.ds(pl.multiple_of(piece * LANES, LANES), LANES)],
            dst_ref=halo.at[side, piece, pl.ds(part * cut, cut)],
            send_sem=halo_send.at[side], recv_sem=halo_recv.at[side, piece, part],
            device_id=target, device_id_type=MESH)

    def share_copy(piece, part, of, target, send, recv):
        block = dz.at[piece, pl.ds(of * quarter + part * cut, cut)]
        return pltpu.make_async_remote_copy(
            src_ref=block, dst_ref=block, send_sem=send, recv_sem=recv.at[piece, part],
            device_id={"rcv": target}, device_id_type=MESH)

    def to_sibling(piece, part):
        return share_copy(piece, part, rcv, sibling, sib_send, sib_recv)

    def to_partner(piece, part):
        return share_copy(piece, part, rcv, partner, par_send, par_recv)

    def forward(piece, part):
        return share_copy(piece, part, partner, sibling, fwd_send, fwd_recv)

    def red_copy(which, piece):
        target = (sibling, partner, diagonal)[which]
        return pltpu.make_async_remote_copy(
            src_ref=kpart.at[piece, target], dst_ref=red.at[which, piece],
            send_sem=red_send, recv_sem=red_recv.at[which],
            device_id={"rcv": target}, device_id_type=MESH)

    def send_halo(side):
        for piece in range(pieces):
            for part in range(CUTS):
                halo_copy(side, piece, part).start()

    at_sides(has_above, has_below, send_halo)

    def blank(side):
        halo[side] = jnp.zeros(halo.shape[1:], BF16)

    at_sides(slab == 0, slab == slabs - 1, blank)

    a, b = iota2((slots, stations * snaps), 0), iota2((slots, stations * snaps), 1)
    lag = (a & (snaps - 1)) - (b & (snaps - 1)) + lags // 2
    taps = jnp.zeros((slots, stations * snaps), F32)
    for source in range(sources):
        for station in range(stations):
            used = pairs[source, station].astype(F32)
            here = ((a // snaps) == source) & ((b // snaps) == station)
            for j in range(lags):
                taps = taps + jnp.where(here & (lag == j), filt[source, station, j] * used, 0.0)
    high = taps.astype(BF16)
    low = (taps - high.astype(F32)).astype(BF16)
    size, depth = slots * HALF, stations * snaps * HALF
    spread = ((iota2((size, slots), 0) >> 3) == iota2((size, slots), 1)).astype(BF16)
    spread_t = (iota2((stations * snaps, depth), 0) == (iota2((stations * snaps, depth), 1) >> 3)).astype(BF16)
    same_row = ((iota2((size, depth), 0) ^ iota2((size, depth), 1)) & (HALF - 1)) == 0
    for n, part in enumerate((high, low)):
        tall = jnp.dot(spread, part, preferred_element_type=F32).astype(BF16)
        mixer[n * size:(n + 1) * size] = jnp.where(
            same_row, jnp.dot(tall, spread_t, preferred_element_type=F32), 0.0).astype(BF16)
    i, o = iota2(colmat.shape, 0), iota2(colmat.shape, 1)
    colmat[...] = stencil(i - LANES - o).astype(BF16)
    i, o = iota2(rowmat.shape, 1), iota2(rowmat.shape, 0)
    rowmat[...] = jnp.where((i >> 4) == (o >> 4), stencil(i - o), 0.0).astype(BF16)
    lam_copy.wait()
    mu_copy.wait()

    half = slots // 2

    def early(step):
        block, plane = step // 2, step % 2
        slot = block % 2

        @pl.when(plane == 0)
        def _():
            g_copy(block).wait()

        for c in range(6):
            g = gv[block, :, c, plane].astype(F32)
            for part in range(2):
                rows = g[:, part * HALF:(part + 1) * HALF].reshape(depth, WIDE).astype(BF16)
                both = jnp.dot(mixer[...], rows, preferred_element_type=F32)
                hbuf[c, part] = both[:size] + both[size:]
        start = pl.multiple_of(block * WIDE, WIDE)

        @pl.when(step == 0)
        def _():
            edge = jnp.zeros(uv.shape[:-1] + (LANES,), BF16)
            u_copy.wait()
            uv[:, :, :, :, :LANES] = edge
            uv[:, :, :, :, LANES + cols:] = edge

        for k in range(3):
            around = uv[:, k, plane, :, pl.ds(start, 2 * WIDE)].reshape(slots * ROW, 2 * WIDE)
            dxb[k] = jnp.dot(around, colmat[...], preferred_element_type=F32)
            inside = pl.ds(pl.multiple_of(start + LANES, LANES), WIDE)
            for part in range(2):
                rows = uv[part * half:(part + 1) * half, k, plane, :, inside].reshape(half * ROW, WIDE)
                dyb[k, part * half * ROW:(part + 1) * half * ROW] = jnp.dot(
                    rowmat[...], rows, preferred_element_type=F32)
        lam = lamv[plane, :, pl.ds(start, WIDE)]
        shear = 2.0 * muv[plane, :, pl.ds(start, WIDE)]

        for source in range(sources):
            def weigh(t, carry):
                trace, rest = carry
                at = source * snaps + t
                here = pl.ds(pl.multiple_of(at * ROW, ROW), ROW)
                rows = pl.ds(pl.multiple_of(at * HALF, HALF), HALF)
                h = [jnp.concatenate([hbuf[c, 0, rows], hbuf[c, 1, rows]], axis=0) for c in range(6)]
                dx = [dxb[k, here] for k in range(3)]
                dy = [dyb[k, here] for k in range(3)]
                total = h[0] + h[1] + h[2]
                trace = trace + (dx[0] + dy[1]) * total
                rest = rest + (dx[0] * h[0] + dy[1] * h[1] + dy[2] * h[3] + dx[2] * h[4] + (dy[0] + dx[1]) * h[5])
                for k, value in enumerate((shear * h[4], shear * h[3], lam * total + shear * h[2])):
                    for side in range(2):
                        adj[slot, side, k, at, plane] = value[:, side * LANES:(side + 1) * LANES]
                return trace, rest

            zero = jnp.zeros((ROW, WIDE), F32)
            trace, rest = lax.fori_loop(0, snaps, weigh, (zero, zero), unroll=2)
            value = lam * trace + shear * rest
            for side in range(2):
                kacc[2 * block + side, source, plane] = value[:, side * LANES:(side + 1) * LANES]

    def depth_derivative(piece, part):
        here = pl.ds(pl.multiple_of(LANES + piece * LANES, LANES), LANES)

        def one(n, _):
            n = part * cut + n
            at = rcv * quarter + n
            for k in range(3):
                f0, f1 = (uv[at, k, plane, :, here].astype(F32) for plane in range(2))
                b0, b1 = (halo[0, piece, n, k, plane].astype(F32) for plane in range(2))
                a0, a1 = (halo[1, piece, n, k, plane].astype(F32) for plane in range(2))
                dz[piece, at, k, 0] = (8.0 * (f1 - b1) - (a0 - b0)).astype(BF16)
                dz[piece, at, k, 1] = (8.0 * (a0 - f0) - (a1 - b1)).astype(BF16)
            return 0

        lax.fori_loop(0, cut, one, 0, unroll=True)

    def late(piece, of):
        slot, side = (piece // 2) % 2, piece % 2
        source = of * quarter // snaps

        def add(n, totals):
            at = of * quarter + n
            new = []
            for plane in range(2):
                terms = [dz[piece, at, k, plane].astype(F32) * adj[slot, side, k, at, plane] for k in range(3)]
                new.append(totals[plane] + (terms[0] + terms[1] + terms[2]))
            return tuple(new)

        totals = lax.fori_loop(0, quarter, add, tuple(kacc[piece, source, plane] for plane in range(2)), unroll=True)
        for plane in range(2):
            kacc[piece, source, plane] = totals[plane]

    def hand_out(piece):
        for source in range(sources):
            for plane in range(2):
                value = kacc[piece, source, plane] * (1.0 / 12.0)
                for owner in range(4):
                    kpart[piece, owner, source, plane] = value[owner * (ROW // 4):(owner + 1) * (ROW // 4)]
        for which in range(3):
            red_copy(which, piece).start()

    def step(s, _):
        @pl.when(s < pieces)
        def _():
            early(s)
            for part in range(CUTS):
                at_sides(has_below, has_above, lambda side: halo_copy(side, s, part).wait_recv())
                depth_derivative(s, part)
                to_partner(s, part).start()
                to_sibling(s, part).start()

        @pl.when(s >= 2)
        def _():
            for part in range(CUTS):
                to_sibling(s - 2, part).wait_recv()
            for of in (rcv, sibling, partner):
                late(s - 2, of)
            for part in range(CUTS):
                forward(s - 2, part).wait_recv()
            late(s - 2, diagonal)
            hand_out(s - 2)

        @pl.when((s >= 1) & (s <= pieces))
        def _():
            for part in range(CUTS):
                to_partner(s - 1, part).wait_recv()
                forward(s - 1, part).start()
        return 0

    lax.fori_loop(0, pieces + 2, step, 0)

    def all_sent(block, sem):
        pltpu.make_async_remote_copy(
            src_ref=block, dst_ref=block, send_sem=sem, recv_sem=sem,
            device_id={"rcv": sibling}, device_id_type=MESH).wait_send()

    at_sides(has_above, has_below, lambda side: all_sent(halo.at[side], halo_send.at[side]))
    for sem in (sib_send, par_send, fwd_send):
        all_sent(dz.at[:, pl.ds(rcv * quarter, quarter)], sem)
    all_sent(red, red_send)
    for which in range(3):
        pltpu.make_async_copy(red.at[which], red.at[which], red_recv.at[which]).wait()
    for piece in range(pieces):
        out_ref[:, :, :, piece * LANES:(piece + 1) * LANES] = (
            (kpart[piece, rcv] + red[0, piece]) + (red[1, piece] + red[2, piece]))


def on_device(displacement, green, lame_lambda, shear_modulus, filters, pairs):
    sources, snaps, parts, planes, rows, cols = displacement.shape
    stations, lags = filters.shape[1:]
    slots, taps = sources * snaps, stations * snaps
    pieces, blocks, quarter = cols // LANES, cols // WIDE, slots // 4
    size, depth = slots * ROW, taps * ROW
    anywhere = pl.BlockSpec(memory_space=pl.ANY)
    scalars = pl.BlockSpec(memory_space=pltpu.SMEM)
    dma = pltpu.SemaphoreType.DMA
    return pl.pallas_call(
        functools.partial(kernel, sources, snaps, stations, lags),
        out_shape=jax.ShapeDtypeStruct((sources, planes, rows // 4, cols), F32),
        in_specs=[anywhere] * 4 + [scalars] * 2,
        out_specs=pl.BlockSpec(memory_space=pltpu.VMEM),
        scratch_shapes=[
            pltpu.VMEM((slots, parts, planes, rows, cols + 2 * LANES), BF16),
            pltpu.VMEM((blocks, taps, 6, planes, rows, WIDE), BF16),
            pltpu.VMEM((planes, rows, cols), F32),
            pltpu.VMEM((planes, rows, cols), F32),
            pltpu.VMEM((2, pieces, quarter, parts, planes, rows, LANES), BF16),
            pltpu.VMEM((pieces, slots, parts, planes, rows, LANES), BF16),
            pltpu.VMEM((2, 2, parts, slots, planes, rows, LANES), F32),
            pltpu.VMEM((6, 2, size // 2, WIDE), F32),
            pltpu.VMEM((3, size, WIDE), F32),
            pltpu.VMEM((3, size, WIDE), F32),
            pltpu.VMEM((size, depth // 2), BF16),
            pltpu.VMEM((2 * WIDE, WIDE), BF16),
            pltpu.VMEM((size // 2, size // 2), BF16),
            pltpu.VMEM((pieces, sources, planes, rows, LANES), F32),
            pltpu.VMEM((pieces, 4, sources, planes, rows // 4, LANES), F32),
            pltpu.VMEM((3, pieces, sources, planes, rows // 4, LANES), F32),
            dma, dma((blocks,)), dma, dma,
            dma((2,)), dma((2, pieces, CUTS)),
            dma, dma((pieces, CUTS)), dma, dma((pieces, CUTS)), dma, dma((pieces, CUTS)),
            dma, dma((3,)),
        ],
        compiler_params=pltpu.CompilerParams(
            collective_id=0, has_side_effects=True, vmem_limit_bytes=60 << 20),
        cost_estimate=pl.CostEstimate(flops=26_000_000_000, bytes_accessed=20_000_000, transcendentals=0),
    )(
        displacement.reshape(slots, parts, planes, rows, cols),
        green.reshape(taps, 6, planes, rows, cols),
        lame_lambda, shear_modulus, filters, pairs,
    )


def solution(mesh):
    placed = (
        P(None, None, None, "slab", None, None),
        P("rcv", None, None, "slab", None, None),
        P("slab", None, None),
        P("slab", None, None),
        P(None, "rcv", None),
        P(None, "rcv"),
    )
    return jax.shard_map(
        on_device,
        mesh=mesh,
        in_specs=placed,
        out_specs=P(None, "slab", "rcv", None),
        check_vma=False,
    )
```

```python
import functools

import jax
import jax.numpy as jnp
from jax import lax
from jax.experimental import pallas as pl
from jax.experimental.pallas import tpu as pltpu
from jax.sharding import PartitionSpec as P

MESH = pl.DeviceIdType.MESH
F32, BF16 = jnp.float32, jnp.bfloat16
ROW = 16
LANES = 128
WIDE = 256
RING_X = 4
HALF = ROW // 2
FIRST = 3


def iota2(shape, axis):
    return lax.broadcasted_iota(jnp.int32, shape, axis)


def stencil(offset):
    eight = jnp.where(offset == 1, 8.0, jnp.where(offset == -1, -8.0, 0.0))
    return jnp.where(offset == 2, -1.0, jnp.where(offset == -2, 1.0, eight))


def kernel(
    sources, snaps, stations, lags,
    u_hbm, g_hbm, lam_hbm, mu_hbm, filt, pairs, out_ref,
    uv, gv, lamv, muv, halo, adj, from_sib, to_par, from_par, hbuf, dxb, dyb, mixer, colmat, rowmat, kacc, kpart, red,
    u_sem, g_sem, lam_sem, mu_sem,
    halo_send, halo_recv, sib_send, sib_recv, par_send, par_recv, red_send, red_recv,
):
    slots = sources * snaps
    quarter = slots // 4
    pieces = halo.shape[1]
    blocks = gv.shape[0]
    steps = adj.shape[0]
    cols = u_hbm.shape[-1]

    rcv, slab = lax.axis_index("rcv"), lax.axis_index("slab")
    slabs = lax.axis_size("slab")
    sibling = rcv + 1 - 2 * (rcv % 2)
    partner = (rcv + 2) % 4
    diagonal = (sibling + 2) % 4
    core, chip = rcv % 2, rcv // 2

    def first_of(device):
        return device % 2 * snaps + device // 2 * quarter

    up_rcv = (rcv + 2 * ((slab % RING_X + 1) // RING_X)) % 4
    down_rcv = (rcv + 2 * ((RING_X - slab % RING_X) // RING_X)) % 4
    up = {"slab": (slab + 1) % slabs, "rcv": up_rcv}
    down = {"slab": (slab + slabs - 1) % slabs, "rcv": down_rcv}
    has_above, has_below = slab < slabs - 1, slab > 0
    count_above, count_below = (2 * slabs - 2 - slab) // slabs, (slabs - 1 + slab) // slabs

    u_copy = pltpu.make_async_copy(u_hbm, uv.at[:, :, :, :, pl.ds(LANES, cols)], u_sem)

    def g_copy(step):
        block, plane = step // 2, step % 2
        return pltpu.make_async_copy(
            g_hbm.at[:, :, plane, :, pl.ds(pl.multiple_of(block * WIDE, WIDE), WIDE)], gv.at[block, :, :, plane],
            g_sem.at[step])

    g_copy(0).start()
    lam_copy = pltpu.make_async_copy(lam_hbm, lamv, lam_sem)
    mu_copy = pltpu.make_async_copy(mu_hbm, muv, mu_sem)
    lam_copy.start()
    mu_copy.start()

    barrier = pltpu.get_barrier_semaphore()
    def greet(peer):
        pl.semaphore_signal(barrier, inc=1, device_id=peer, device_id_type=MESH)

    def at_sides(condition_up, condition_down, act):
        for side, condition in enumerate((condition_up, condition_down)):
            @pl.when(condition)
            def _(side=side):
                act(side)

    at_sides(has_above, has_below, lambda side: greet((up, down)[side]))
    for peer in (sibling, partner, diagonal):
        greet({"rcv": peer})
    def halo_copy(side, piece):
        target, their = ((up, up_rcv), (down, down_rcv))[side]
        return pltpu.make_async_remote_copy(
            src_ref=u_hbm.at[pl.ds(first_of(their), quarter), :, :, :, pl.ds(pl.multiple_of(piece * LANES, LANES), LANES)],
            dst_ref=halo.at[side, piece], send_sem=halo_send.at[side], recv_sem=halo_recv.at[side, piece],
            device_id=target, device_id_type=MESH)

    def to_sibling(step, whose):
        half_of = pl.ds((chip + whose - 2 * chip * whose) * quarter, quarter)
        return pltpu.make_async_remote_copy(
            src_ref=adj.at[step, 1 - core, :, half_of], dst_ref=from_sib.at[step, :, half_of],
            send_sem=sib_send, recv_sem=sib_recv.at[step, whose],
            device_id={"rcv": sibling}, device_id_type=MESH)

    def to_partner(step):
        return pltpu.make_async_remote_copy(
            src_ref=to_par.at[step], dst_ref=from_par.at[step], send_sem=par_send, recv_sem=par_recv.at[step],
            device_id={"rcv": partner}, device_id_type=MESH)

    def red_copy(which, piece):
        target = (sibling, partner, diagonal)[which]
        return pltpu.make_async_remote_copy(
            src_ref=kpart.at[piece, target], dst_ref=red.at[which, piece],
            send_sem=red_send, recv_sem=red_recv.at[which],
            device_id={"rcv": target}, device_id_type=MESH)

    a, b = iota2((slots, stations * snaps), 0), iota2((slots, stations * snaps), 1)
    lag = (a & (snaps - 1)) - (b & (snaps - 1)) + lags // 2
    taps = jnp.zeros((slots, stations * snaps), F32)
    for source in range(sources):
        for station in range(stations):
            used = pairs[source, station].astype(F32)
            here = ((a // snaps) == source) & ((b // snaps) == station)
            for j in range(lags):
                taps = taps + jnp.where(here & (lag == j), filt[source, station, j] * used, 0.0)
    high = taps.astype(BF16)
    low = (taps - high.astype(F32)).astype(BF16)
    size, depth = slots * HALF, stations * snaps * HALF
    spread = ((iota2((size, slots), 0) >> 3) == iota2((size, slots), 1)).astype(BF16)
    spread_t = (iota2((stations * snaps, depth), 0) == (iota2((stations * snaps, depth), 1) >> 3)).astype(BF16)
    same_row = ((iota2((size, depth), 0) ^ iota2((size, depth), 1)) & (HALF - 1)) == 0
    for n, part in enumerate((high, low)):
        tall = jnp.dot(spread, part, preferred_element_type=F32).astype(BF16)
        mixer[n * size:(n + 1) * size] = jnp.where(
            same_row, jnp.dot(tall, spread_t, preferred_element_type=F32), 0.0).astype(BF16)

    pl.semaphore_wait(barrier, 3 + count_above + count_below)

    def send_halo(first, last):
        def send(side):
            for piece in range(first, last):
                halo_copy(side, piece).start()

        at_sides(has_above, has_below, send)

    def blank(side):
        halo[side] = jnp.zeros(halo.shape[1:], BF16)

    send_halo(0, FIRST)
    lam_copy.wait()
    mu_copy.wait()

    half = slots // 2

    def early(step):
        block, plane = step // 2, step % 2

        g_copy(step).wait()

        @pl.when(step == 0)
        def _():
            u_copy.start()

        @pl.when(step + 1 < steps)
        def _():
            g_copy(step + 1).start()

        for c in range(6):
            g = gv[block, :, c, plane].astype(F32)
            for part in range(2):
                rows = g[:, part * HALF:(part + 1) * HALF].reshape(depth, WIDE).astype(BF16)
                both = jnp.dot(mixer[...], rows, preferred_element_type=F32)
                hbuf[c, part] = both[:size] + both[size:]
        start = pl.multiple_of(block * WIDE, WIDE)
        lam = lamv[plane, :, pl.ds(start, WIDE)]
        shear = 2.0 * muv[plane, :, pl.ds(start, WIDE)]

        def mixed(c, at):
            rows = pl.ds(pl.multiple_of(at * HALF, HALF), HALF)
            return jnp.concatenate([hbuf[c, 0, rows], hbuf[c, 1, rows]], axis=0)

        for source in range(sources):
            def turn(t, _):
                h = [mixed(c, source * snaps + t) for c in range(5)]
                adj[step, source, 0, t] = shear * h[4]
                adj[step, source, 1, t] = shear * h[3]
                adj[step, source, 2, t] = lam * (h[0] + h[1] + h[2]) + shear * h[2]
                return 0

            lax.fori_loop(0, snaps, turn, 0, unroll=2)
        to_sibling(step, 1).start()
        to_sibling(step, 0).start()

        @pl.when(step == 0)
        def _():
            send_halo(FIRST, pieces)
            at_sides(slab == 0, slab == slabs - 1, blank)
            i, o = iota2(colmat.shape, 0), iota2(colmat.shape, 1)
            colmat[...] = stencil(i - LANES - o).astype(BF16)
            i, o = iota2(rowmat.shape, 1), iota2(rowmat.shape, 0)
            rowmat[...] = jnp.where((i >> 4) == (o >> 4), stencil(i - o), 0.0).astype(BF16)
            edge = jnp.zeros(uv.shape[:-1] + (LANES,), BF16)
            u_copy.wait()
            uv[:, :, :, :, :LANES] = edge
            uv[:, :, :, :, LANES + cols:] = edge

        for k in range(3):
            around = uv[:, k, plane, :, pl.ds(start, 2 * WIDE)].reshape(slots * ROW, 2 * WIDE)
            dxb[k] = jnp.dot(around, colmat[...], preferred_element_type=F32)
            inside = pl.ds(pl.multiple_of(start + LANES, LANES), WIDE)
            for part in range(2):
                rows = uv[part * half:(part + 1) * half, k, plane, :, inside].reshape(half * ROW, WIDE)
                dyb[k, part * half * ROW:(part + 1) * half * ROW] = jnp.dot(
                    rowmat[...], rows, preferred_element_type=F32)

        to_sibling(step, 1).wait_recv()

        def pass_on(n, _):
            t = (1 - chip) * quarter + n
            for k in range(3):
                to_par[step, k, n] = (adj[step, core, k, t] + from_sib[step, k, t]).astype(BF16)
            return 0

        lax.fori_loop(0, quarter, pass_on, 0, unroll=2)
        to_partner(step).start()

        for source in range(sources):
            def weigh(t, carry):
                trace, rest = carry
                at = source * snaps + t
                here = pl.ds(pl.multiple_of(at * ROW, ROW), ROW)
                h = [mixed(c, at) for c in range(6)]
                dx = [dxb[k, here] for k in range(3)]
                dy = [dyb[k, here] for k in range(3)]
                trace = trace + (dx[0] + dy[1]) * (h[0] + h[1] + h[2])
                rest = rest + (dx[0] * h[0] + dy[1] * h[1] + dy[2] * h[3] + dx[2] * h[4] + (dy[0] + dx[1]) * h[5])
                return trace, rest

            zero = jnp.zeros((ROW, WIDE), F32)
            trace, rest = lax.fori_loop(0, snaps, weigh, (zero, zero), unroll=2)
            value = lam * trace + shear * rest
            for side in range(2):
                kacc[2 * block + side, source, plane] = value[:, side * LANES:(side + 1) * LANES]

    def late(piece):
        block, side = piece // 2, piece % 2
        lanes = pl.ds(pl.multiple_of(side * LANES, LANES), LANES)
        here = pl.ds(pl.multiple_of(LANES + piece * LANES, LANES), LANES)

        def add(n, totals):
            at, t = first_of(rcv) + n, chip * quarter + n
            new = list(totals)
            for k in range(3):
                f0, f1 = (uv[at, k, plane, :, here].astype(F32) for plane in range(2))
                b0, b1 = (halo[0, piece, n, k, plane].astype(F32) for plane in range(2))
                a0, a1 = (halo[1, piece, n, k, plane].astype(F32) for plane in range(2))
                slopes = 8.0 * (f1 - b1) - (a0 - b0), 8.0 * (a0 - f0) - (a1 - b1)
                for plane in range(2):
                    step = 2 * block + plane
                    whole = (adj[step, core, k, t, :, lanes] + from_sib[step, k, t, :, lanes]
                             + from_par[step, k, n, :, lanes].astype(F32))
                    new[plane] = new[plane] + slopes[plane] * whole
            return tuple(new)

        totals = lax.fori_loop(0, quarter, add, tuple(kacc[piece, core, plane] for plane in range(2)), unroll=2)
        for plane in range(2):
            kacc[piece, core, plane] = totals[plane]

    def hand_out(piece):
        for source in range(sources):
            for plane in range(2):
                value = kacc[piece, source, plane] * (1.0 / 12.0)
                for owner in range(4):
                    kpart[piece, owner, source, plane] = value[owner * (ROW // 4):(owner + 1) * (ROW // 4)]
        for which in range(3):
            red_copy(which, piece).start()

    def compute(step, _):
        early(step)
        return 0

    def finish(piece, _):
        @pl.when(piece % 2 == 0)
        def _():
            for plane in range(2):
                to_sibling(2 * (piece // 2) + plane, 0).wait_recv()
                to_partner(2 * (piece // 2) + plane).wait_recv()

        at_sides(has_below, has_above, lambda side: halo_copy(side, piece).wait_recv())
        late(piece)
        hand_out(piece)
        return 0

    lax.fori_loop(0, steps, compute, 0)
    lax.fori_loop(0, pieces, finish, 0)

    def all_sent(block, sem):
        pltpu.make_async_remote_copy(
            src_ref=block, dst_ref=block, send_sem=sem, recv_sem=sem,
            device_id={"rcv": sibling}, device_id_type=MESH).wait_send()

    at_sides(has_above, has_below, lambda side: all_sent(halo.at[side], halo_send.at[side]))
    all_sent(from_sib, sib_send)
    all_sent(from_par, par_send)
    all_sent(red, red_send)
    for which in range(3):
        pltpu.make_async_copy(red.at[which], red.at[which], red_recv.at[which]).wait()
    for piece in range(pieces):
        out_ref[:, :, :, piece * LANES:(piece + 1) * LANES] = (
            (kpart[piece, rcv] + red[0, piece]) + (red[1, piece] + red[2, piece]))


def on_device(displacement, green, lame_lambda, shear_modulus, filters, pairs):
    sources, snaps, parts, planes, rows, cols = displacement.shape
    stations, lags = filters.shape[1:]
    slots, taps = sources * snaps, stations * snaps
    pieces, blocks, quarter = cols // LANES, cols // WIDE, slots // 4
    size, depth, steps = slots * ROW, taps * ROW, blocks * planes
    anywhere = pl.BlockSpec(memory_space=pl.ANY)
    scalars = pl.BlockSpec(memory_space=pltpu.SMEM)
    dma = pltpu.SemaphoreType.DMA
    return pl.pallas_call(
        functools.partial(kernel, sources, snaps, stations, lags),
        out_shape=jax.ShapeDtypeStruct((sources, planes, rows // 4, cols), F32),
        in_specs=[anywhere] * 4 + [scalars] * 2,
        out_specs=pl.BlockSpec(memory_space=pltpu.VMEM),
        scratch_shapes=[
            pltpu.VMEM((slots, parts, planes, rows, cols + 2 * LANES), BF16),
            pltpu.VMEM((blocks, taps, 6, planes, rows, WIDE), BF16),
            pltpu.VMEM((planes, rows, cols), F32),
            pltpu.VMEM((planes, rows, cols), F32),
            pltpu.VMEM((2, pieces, quarter, parts, planes, rows, LANES), BF16),
            pltpu.VMEM((steps, sources, 3, snaps, rows, WIDE), F32),
            pltpu.VMEM((steps, 3, snaps, rows, WIDE), F32),
            pltpu.VMEM((steps, 3, quarter, rows, WIDE), BF16),
            pltpu.VMEM((steps, 3, quarter, rows, WIDE), BF16),
            pltpu.VMEM((6, 2, size // 2, WIDE), F32),
            pltpu.VMEM((3, size, WIDE), F32),
            pltpu.VMEM((3, size, WIDE), F32),
            pltpu.VMEM((size, depth // 2), BF16),
            pltpu.VMEM((2 * WIDE, WIDE), BF16),
            pltpu.VMEM((size // 2, size // 2), BF16),
            pltpu.VMEM((pieces, sources, planes, rows, LANES), F32),
            pltpu.VMEM((pieces, 4, sources, planes, rows // 4, LANES), F32),
            pltpu.VMEM((3, pieces, sources, planes, rows // 4, LANES), F32),
            dma, dma((steps,)), dma, dma,
            dma((2,)), dma((2, pieces)), dma, dma((steps, 2)), dma, dma((steps,)), dma, dma((3,)),
        ],
        compiler_params=pltpu.CompilerParams(
            collective_id=0, has_side_effects=True, vmem_limit_bytes=60 << 20),
        cost_estimate=pl.CostEstimate(flops=26_000_000_000, bytes_accessed=20_000_000, transcendentals=0),
    )(
        displacement.reshape(slots, parts, planes, rows, cols),
        green.reshape(taps, 6, planes, rows, cols),
        lame_lambda, shear_modulus, filters, pairs,
    )


def solution(mesh):
    placed = (
        P(None, None, None, "slab", None, None),
        P("rcv", None, None, "slab", None, None),
        P("slab", None, None),
        P("slab", None, None),
        P(None, "rcv", None),
        P(None, "rcv"),
    )
    return jax.shard_map(
        on_device,
        mesh=mesh,
        in_specs=placed,
        out_specs=P(None, "slab", "rcv", None),
        check_vma=False,
    )
```

```python
import functools

import jax
import jax.numpy as jnp
from jax import lax
from jax.experimental import pallas as pl
from jax.experimental.pallas import tpu as pltpu
from jax.sharding import PartitionSpec as P

MESH = pl.DeviceIdType.MESH
F32, BF16 = jnp.float32, jnp.bfloat16
ROW = 16
LANES = 128
WIDE = 256
RING_X = 4
HALF = ROW // 2
FIRST = 3
EXTRA = 1


def iota2(shape, axis):
    return lax.broadcasted_iota(jnp.int32, shape, axis)


def stencil(offset):
    eight = jnp.where(offset == 1, 8.0, jnp.where(offset == -1, -8.0, 0.0))
    return jnp.where(offset == 2, -1.0, jnp.where(offset == -2, 1.0, eight))


def kernel(
    sources, snaps, stations, lags,
    u_hbm, g_hbm, lam_hbm, mu_hbm, filt, pairs, out_ref,
    uv, gv, lamv, muv, halo, extra, adj, from_sib, to_par, from_par, hbuf, dxb, dyb, mixer, colmat, rowmat, kacc, kpart, red,
    u_sem, g_sem, lam_sem, mu_sem,
    halo_send, halo_recv, extra_send, extra_recv, sib_send, sib_recv, par_send, par_recv, red_send, red_recv,
):
    slots = sources * snaps
    quarter = slots // 4
    pieces = halo.shape[1]
    blocks = gv.shape[0]
    steps = adj.shape[0]
    cols = u_hbm.shape[-1]

    rcv, slab = lax.axis_index("rcv"), lax.axis_index("slab")
    slabs = lax.axis_size("slab")
    sibling = rcv + 1 - 2 * (rcv % 2)
    partner = (rcv + 2) % 4
    diagonal = (sibling + 2) % 4
    core, chip = rcv % 2, rcv // 2

    def first_of(device):
        return device % 2 * snaps + device // 2 * quarter

    def others_of(device):
        return device % 2 * snaps + (1 - device // 2) * quarter

    up_rcv = (rcv + 2 * ((slab % RING_X + 1) // RING_X)) % 4
    down_rcv = (rcv + 2 * ((RING_X - slab % RING_X) // RING_X)) % 4
    up = {"slab": (slab + 1) % slabs, "rcv": up_rcv}
    down = {"slab": (slab + slabs - 1) % slabs, "rcv": down_rcv}
    has_above, has_below = slab < slabs - 1, slab > 0
    count_above, count_below = (2 * slabs - 2 - slab) // slabs, (slabs - 1 + slab) // slabs

    u_copy = pltpu.make_async_copy(u_hbm, uv.at[:, :, :, :, pl.ds(LANES, cols)], u_sem)

    def g_copy(step):
        block, plane = step // 2, step % 2
        return pltpu.make_async_copy(
            g_hbm.at[:, :, plane, :, pl.ds(pl.multiple_of(block * WIDE, WIDE), WIDE)], gv.at[block, :, :, plane],
            g_sem.at[step])

    g_copy(0).start()
    lam_copy = pltpu.make_async_copy(lam_hbm, lamv, lam_sem)
    mu_copy = pltpu.make_async_copy(mu_hbm, muv, mu_sem)
    lam_copy.start()
    mu_copy.start()

    barrier = pltpu.get_barrier_semaphore()
    def greet(peer):
        pl.semaphore_signal(barrier, inc=1, device_id=peer, device_id_type=MESH)

    def at_sides(condition_up, condition_down, act):
        for side, condition in enumerate((condition_up, condition_down)):
            @pl.when(condition)
            def _(side=side):
                act(side)

    at_sides(has_above, has_below, lambda side: greet((up, down)[side]))
    for peer in (sibling, partner, diagonal):
        greet({"rcv": peer})
    def halo_copy(side, piece):
        target, their = ((up, up_rcv), (down, down_rcv))[side]
        return pltpu.make_async_remote_copy(
            src_ref=u_hbm.at[pl.ds(first_of(their), quarter), :, :, :, pl.ds(pl.multiple_of(piece * LANES, LANES), LANES)],
            dst_ref=halo.at[side, piece], send_sem=halo_send.at[side], recv_sem=halo_recv.at[side, piece],
            device_id=target, device_id_type=MESH)

    def extra_copy(side, n):
        target, their = ((up, up_rcv), (down, down_rcv))[side]
        return pltpu.make_async_remote_copy(
            src_ref=u_hbm.at[pl.ds(others_of(their), EXTRA), :, :, :, pl.ds((pieces - 2 + n) * LANES, LANES)],
            dst_ref=extra.at[side, n], send_sem=extra_send.at[side], recv_sem=extra_recv.at[side, n],
            device_id=target, device_id_type=MESH)

    def to_sibling(step, whose):
        half_of = pl.ds((chip + whose - 2 * chip * whose) * quarter, quarter)
        return pltpu.make_async_remote_copy(
            src_ref=adj.at[step, 1 - core, :, half_of], dst_ref=from_sib.at[step, :, half_of],
            send_sem=sib_send, recv_sem=sib_recv.at[step, whose],
            device_id={"rcv": sibling}, device_id_type=MESH)

    def to_partner(step, skip):
        part = pl.ds(skip, quarter - skip)
        return pltpu.make_async_remote_copy(
            src_ref=to_par.at[step, :, part], dst_ref=from_par.at[step, :, part],
            send_sem=par_send.at[min(skip, 1)], recv_sem=par_recv.at[step],
            device_id={"rcv": partner}, device_id_type=MESH)

    def red_copy(which, piece):
        target = (sibling, partner, diagonal)[which]
        return pltpu.make_async_remote_copy(
            src_ref=kpart.at[piece, target], dst_ref=red.at[which, piece],
            send_sem=red_send, recv_sem=red_recv.at[which],
            device_id={"rcv": target}, device_id_type=MESH)

    a, b = iota2((slots, stations * snaps), 0), iota2((slots, stations * snaps), 1)
    lag = (a & (snaps - 1)) - (b & (snaps - 1)) + lags // 2
    taps = jnp.zeros((slots, stations * snaps), F32)
    for source in range(sources):
        for station in range(stations):
            used = pairs[source, station].astype(F32)
            here = ((a // snaps) == source) & ((b // snaps) == station)
            for j in range(lags):
                taps = taps + jnp.where(here & (lag == j), filt[source, station, j] * used, 0.0)
    high = taps.astype(BF16)
    low = (taps - high.astype(F32)).astype(BF16)
    size, depth = slots * HALF, stations * snaps * HALF
    spread = ((iota2((size, slots), 0) >> 3) == iota2((size, slots), 1)).astype(BF16)
    spread_t = (iota2((stations * snaps, depth), 0) == (iota2((stations * snaps, depth), 1) >> 3)).astype(BF16)
    same_row = ((iota2((size, depth), 0) ^ iota2((size, depth), 1)) & (HALF - 1)) == 0
    for n, part in enumerate((high, low)):
        tall = jnp.dot(spread, part, preferred_element_type=F32).astype(BF16)
        mixer[n * size:(n + 1) * size] = jnp.where(
            same_row, jnp.dot(tall, spread_t, preferred_element_type=F32), 0.0).astype(BF16)

    pl.semaphore_wait(barrier, 3 + count_above + count_below)

    def send_halo(first, last):
        def send(side):
            for piece in range(first, last):
                halo_copy(side, piece).start()
            if last == pieces:
                for n in range(2):
                    extra_copy(side, n).start()

        at_sides(has_above, has_below, send)

    def blank(side):
        halo[side] = jnp.zeros(halo.shape[1:], BF16)
        extra[side] = jnp.zeros(extra.shape[1:], BF16)

    send_halo(0, min(FIRST, pieces))
    lam_copy.wait()
    mu_copy.wait()

    half = slots // 2

    def early(step):
        block, plane = step // 2, step % 2

        g_copy(step).wait()

        @pl.when(step == 0)
        def _():
            u_copy.start()

        @pl.when(step + 1 < steps)
        def _():
            g_copy(step + 1).start()

        def mix(c):
            g = gv[block, :, c, plane].astype(F32)
            for part in range(2):
                rows = g[:, part * HALF:(part + 1) * HALF].reshape(depth, WIDE).astype(BF16)
                both = jnp.dot(mixer[...], rows, preferred_element_type=F32)
                hbuf[c, part] = both[:size] + both[size:]

        for c in range(5):
            mix(c)
        start = pl.multiple_of(block * WIDE, WIDE)
        lam = lamv[plane, :, pl.ds(start, WIDE)]
        shear = 2.0 * muv[plane, :, pl.ds(start, WIDE)]

        def mixed(c, at):
            rows = pl.ds(pl.multiple_of(at * HALF, HALF), HALF)
            return jnp.concatenate([hbuf[c, 0, rows], hbuf[c, 1, rows]], axis=0)

        for source in range(sources):
            def turn(t, _):
                h = [mixed(c, source * snaps + t) for c in range(5)]
                adj[step, source, 0, t] = shear * h[4]
                adj[step, source, 1, t] = shear * h[3]
                adj[step, source, 2, t] = lam * (h[0] + h[1] + h[2]) + shear * h[2]
                return 0

            lax.fori_loop(0, snaps, turn, 0, unroll=4)
        to_sibling(step, 1).start()
        to_sibling(step, 0).start()

        def share():
            to_sibling(step, 1).wait_recv()

            def pass_on(n, _):
                t = (1 - chip) * quarter + n
                for k in range(3):
                    to_par[step, k, n] = (adj[step, core, k, t] + from_sib[step, k, t]).astype(BF16)
                return 0

            lax.fori_loop(0, quarter, pass_on, 0, unroll=4)

            @pl.when(step < steps - 2)
            def _():
                to_partner(step, 0).start()

            @pl.when(step >= steps - 2)
            def _():
                to_partner(step, EXTRA).start()

        mix(5)

        @pl.when(step == 0)
        def _():
            send_halo(min(FIRST, pieces), pieces)
            at_sides(slab == 0, slab == slabs - 1, blank)
            i, o = iota2(colmat.shape, 0), iota2(colmat.shape, 1)
            colmat[...] = stencil(i - LANES - o).astype(BF16)
            i, o = iota2(rowmat.shape, 1), iota2(rowmat.shape, 0)
            rowmat[...] = jnp.where((i >> 4) == (o >> 4), stencil(i - o), 0.0).astype(BF16)
            edge = jnp.zeros(uv.shape[:-1] + (LANES,), BF16)
            share()
            u_copy.wait()
            uv[:, :, :, :, :LANES] = edge
            uv[:, :, :, :, LANES + cols:] = edge

        for k in range(3):
            around = uv[:, k, plane, :, pl.ds(start, 2 * WIDE)].reshape(slots * ROW, 2 * WIDE)
            dxb[k] = jnp.dot(around, colmat[...], preferred_element_type=F32)
            inside = pl.ds(pl.multiple_of(start + LANES, LANES), WIDE)
            for part in range(2):
                rows = uv[part * half:(part + 1) * half, k, plane, :, inside].reshape(half * ROW, WIDE)
                dyb[k, part * half * ROW:(part + 1) * half * ROW] = jnp.dot(
                    rowmat[...], rows, preferred_element_type=F32)

        @pl.when(step > 0)
        def _():
            share()

        for source in range(sources):
            def weigh(t, carry):
                trace, rest = carry
                at = source * snaps + t
                here = pl.ds(pl.multiple_of(at * ROW, ROW), ROW)
                h = [mixed(c, at) for c in range(6)]
                dx = [dxb[k, here] for k in range(3)]
                dy = [dyb[k, here] for k in range(3)]
                trace = trace + (dx[0] + dy[1]) * (h[0] + h[1] + h[2])
                rest = rest + (dx[0] * h[0] + dy[1] * h[1] + dy[2] * h[3] + dx[2] * h[4] + (dy[0] + dx[1]) * h[5])
                return trace, rest

            zero = jnp.zeros((ROW, WIDE), F32)
            trace, rest = lax.fori_loop(0, snaps, weigh, (zero, zero), unroll=2)
            value = lam * trace + shear * rest
            for side in range(2):
                kacc[2 * block + side, source, plane] = value[:, side * LANES:(side + 1) * LANES]

    def late(piece, last):
        block, side = piece // 2, piece % 2
        lanes = pl.ds(pl.multiple_of(side * LANES, LANES), LANES)
        here = pl.ds(pl.multiple_of(LANES + piece * LANES, LANES), LANES)

        def add(totals, at, t, near, n, handed):
            new = list(totals)
            for k in range(3):
                f0, f1 = (uv[at, k, plane, :, here].astype(F32) for plane in range(2))
                b0, b1 = (near(0)[n, k, plane].astype(F32) for plane in range(2))
                a0, a1 = (near(1)[n, k, plane].astype(F32) for plane in range(2))
                slopes = 8.0 * (f1 - b1) - (a0 - b0), 8.0 * (a0 - f0) - (a1 - b1)
                for plane in range(2):
                    step = 2 * block + plane
                    whole = adj[step, core, k, t, :, lanes] + from_sib[step, k, t, :, lanes]
                    if handed:
                        whole = whole + from_par[step, k, n, :, lanes].astype(F32)
                    new[plane] = new[plane] + slopes[plane] * whole
            return tuple(new)

        def mine(n, totals, handed=True):
            return add(totals, first_of(rcv) + n, chip * quarter + n, lambda s: halo.at[s, piece], n, handed)

        totals = tuple(kacc[piece, core, plane] for plane in range(2))
        if last:
            for n in range(EXTRA):
                totals = mine(n, totals, False)
                totals = add(totals, others_of(rcv) + n, (1 - chip) * quarter + n, lambda s: extra.at[s, side], n, False)
        totals = lax.fori_loop(EXTRA if last else 0, quarter, mine, totals, unroll=True if last else 2)
        for plane in range(2):
            kacc[piece, core, plane] = totals[plane]

    def hand_out(piece):
        for source in range(sources):
            for plane in range(2):
                value = kacc[piece, source, plane] * (1.0 / 12.0)
                for owner in range(4):
                    kpart[piece, owner, source, plane] = value[owner * (ROW // 4):(owner + 1) * (ROW // 4)]
        for which in range(3):
            red_copy(which, piece).start()

    def compute(step, _):
        early(step)
        return 0

    def wait_adjoint(block, skip):
        for plane in range(2):
            to_sibling(2 * block + plane, 0).wait_recv()
            to_partner(2 * block + plane, skip).wait_recv()

    def finish(piece, _):
        @pl.when(piece % 2 == 0)
        def _():
            wait_adjoint(piece // 2, 0)

        at_sides(has_below, has_above, lambda side: halo_copy(side, piece).wait_recv())
        late(piece, False)
        hand_out(piece)
        return 0

    lax.fori_loop(0, steps, compute, 0)
    lax.fori_loop(0, pieces - 2, finish, 0)
    wait_adjoint(blocks - 1, EXTRA)
    for n in range(2):
        def wait_halo(side):
            halo_copy(side, pieces - 2 + n).wait_recv()
            extra_copy(side, n).wait_recv()

        at_sides(has_below, has_above, wait_halo)
        late(pieces - 2 + n, True)
        hand_out(pieces - 2 + n)

    def all_sent(block, sem):
        pltpu.make_async_remote_copy(
            src_ref=block, dst_ref=block, send_sem=sem, recv_sem=sem,
            device_id={"rcv": sibling}, device_id_type=MESH).wait_send()

    at_sides(has_above, has_below, lambda side: all_sent(halo.at[side], halo_send.at[side]))
    all_sent(from_sib, sib_send)
    at_sides(has_above, has_below, lambda side: all_sent(extra.at[side], extra_send.at[side]))
    all_sent(from_par.at[pl.ds(0, steps - 2)], par_send.at[0])
    all_sent(from_par.at[pl.ds(steps - 2, 2), :, pl.ds(EXTRA, quarter - EXTRA)], par_send.at[1])
    all_sent(red, red_send)
    for which in range(3):
        pltpu.make_async_copy(red.at[which], red.at[which], red_recv.at[which]).wait()
    for piece in range(pieces):
        out_ref[:, :, :, piece * LANES:(piece + 1) * LANES] = (
            (kpart[piece, rcv] + red[0, piece]) + (red[1, piece] + red[2, piece]))


def on_device(displacement, green, lame_lambda, shear_modulus, filters, pairs):
    sources, snaps, parts, planes, rows, cols = displacement.shape
    stations, lags = filters.shape[1:]
    slots, taps = sources * snaps, stations * snaps
    pieces, blocks, quarter = cols // LANES, cols // WIDE, slots // 4
    size, depth, steps = slots * ROW, taps * ROW, blocks * planes
    anywhere = pl.BlockSpec(memory_space=pl.ANY)
    scalars = pl.BlockSpec(memory_space=pltpu.SMEM)
    dma = pltpu.SemaphoreType.DMA
    return pl.pallas_call(
        functools.partial(kernel, sources, snaps, stations, lags),
        out_shape=jax.ShapeDtypeStruct((sources, planes, rows // 4, cols), F32),
        in_specs=[anywhere] * 4 + [scalars] * 2,
        out_specs=pl.BlockSpec(memory_space=pltpu.VMEM),
        scratch_shapes=[
            pltpu.VMEM((slots, parts, planes, rows, cols + 2 * LANES), BF16),
            pltpu.VMEM((blocks, taps, 6, planes, rows, WIDE), BF16),
            pltpu.VMEM((planes, rows, cols), F32),
            pltpu.VMEM((planes, rows, cols), F32),
            pltpu.VMEM((2, pieces, quarter, parts, planes, rows, LANES), BF16),
            pltpu.VMEM((2, 2, EXTRA, parts, planes, rows, LANES), BF16),
            pltpu.VMEM((steps, sources, 3, snaps, rows, WIDE), F32),
            pltpu.VMEM((steps, 3, snaps, rows, WIDE), F32),
            pltpu.VMEM((steps, 3, quarter, rows, WIDE), BF16),
            pltpu.VMEM((steps, 3, quarter, rows, WIDE), BF16),
            pltpu.VMEM((6, 2, size // 2, WIDE), F32),
            pltpu.VMEM((3, size, WIDE), F32),
            pltpu.VMEM((3, size, WIDE), F32),
            pltpu.VMEM((size, depth // 2), BF16),
            pltpu.VMEM((2 * WIDE, WIDE), BF16),
            pltpu.VMEM((size // 2, size // 2), BF16),
            pltpu.VMEM((pieces, sources, planes, rows, LANES), F32),
            pltpu.VMEM((pieces, 4, sources, planes, rows // 4, LANES), F32),
            pltpu.VMEM((3, pieces, sources, planes, rows // 4, LANES), F32),
            dma, dma((steps,)), dma, dma,
            dma((2,)), dma((2, pieces)), dma((2,)), dma((2, 2)), dma, dma((steps, 2)), dma((2,)), dma((steps,)),
            dma, dma((3,)),
        ],
        compiler_params=pltpu.CompilerParams(
            collective_id=0, has_side_effects=True, vmem_limit_bytes=60 << 20),
        cost_estimate=pl.CostEstimate(flops=26_000_000_000, bytes_accessed=20_000_000, transcendentals=0),
    )(
        displacement.reshape(slots, parts, planes, rows, cols),
        green.reshape(taps, 6, planes, rows, cols),
        lame_lambda, shear_modulus, filters, pairs,
    )


def solution(mesh):
    placed = (
        P(None, None, None, "slab", None, None),
        P("rcv", None, None, "slab", None, None),
        P("slab", None, None),
        P("slab", None, None),
        P(None, "rcv", None),
        P(None, "rcv"),
    )
    return jax.shard_map(
        on_device,
        mesh=mesh,
        in_specs=placed,
        out_specs=P(None, "slab", "rcv", None),
        check_vma=False,
    )
```

```python
import functools

import jax
import jax.numpy as jnp
from jax import lax
from jax.experimental import pallas as pl
from jax.experimental.pallas import tpu as pltpu
from jax.sharding import PartitionSpec as P

MESH = pl.DeviceIdType.MESH
F32, BF16 = jnp.float32, jnp.bfloat16
ROW = 16
LANES = 128
WIDE = 256
RING_X = 4
HALF = ROW // 2
FIRST = 3
EXTRA = 1


def iota2(shape, axis):
    return lax.broadcasted_iota(jnp.int32, shape, axis)


def stencil(offset):
    eight = jnp.where(offset == 1, 8.0, jnp.where(offset == -1, -8.0, 0.0))
    return jnp.where(offset == 2, -1.0, jnp.where(offset == -2, 1.0, eight))


def kernel(
    sources, snaps, stations, lags,
    u_hbm, g_hbm, lam_hbm, mu_hbm, filt, pairs, out_ref,
    uv, gv, lamv, muv, halo, extra, adj, from_sib, to_par, from_par, hbuf, dxb, dyb, mixer, colmat, rowmat, kacc, kpart, red,
    u_sem, g_sem, lam_sem, mu_sem,
    halo_send, halo_recv, extra_send, extra_recv, sib_send, sib_recv, par_send, par_recv, red_send, red_recv,
):
    slots = sources * snaps
    quarter = slots // 4
    pieces = halo.shape[1]
    blocks = gv.shape[0]
    steps = adj.shape[0]
    cols = u_hbm.shape[-1]

    rcv, slab = lax.axis_index("rcv"), lax.axis_index("slab")
    slabs = lax.axis_size("slab")
    sibling = rcv + 1 - 2 * (rcv % 2)
    partner = (rcv + 2) % 4
    diagonal = (sibling + 2) % 4
    core, chip = rcv % 2, rcv // 2

    def first_of(device):
        return device % 2 * snaps + device // 2 * quarter

    def others_of(device):
        return device % 2 * snaps + (1 - device // 2) * quarter

    up_rcv = (rcv + 2 * ((slab % RING_X + 1) // RING_X)) % 4
    down_rcv = (rcv + 2 * ((RING_X - slab % RING_X) // RING_X)) % 4
    up = {"slab": (slab + 1) % slabs, "rcv": up_rcv}
    down = {"slab": (slab + slabs - 1) % slabs, "rcv": down_rcv}
    has_above, has_below = slab < slabs - 1, slab > 0
    count_above, count_below = (2 * slabs - 2 - slab) // slabs, (slabs - 1 + slab) // slabs

    u_copy = pltpu.make_async_copy(u_hbm, uv.at[:, :, :, :, pl.ds(LANES, cols)], u_sem)

    def g_copy(step):
        block, plane = step // 2, step % 2
        return pltpu.make_async_copy(
            g_hbm.at[:, :, plane, :, pl.ds(pl.multiple_of(block * WIDE, WIDE), WIDE)], gv.at[block, :, :, plane],
            g_sem.at[step])

    g_copy(0).start()
    lam_copy = pltpu.make_async_copy(lam_hbm, lamv, lam_sem)
    mu_copy = pltpu.make_async_copy(mu_hbm, muv, mu_sem)
    lam_copy.start()
    mu_copy.start()

    barrier = pltpu.get_barrier_semaphore()
    def greet(peer):
        pl.semaphore_signal(barrier, inc=1, device_id=peer, device_id_type=MESH)

    def at_sides(condition_up, condition_down, act):
        for side, condition in enumerate((condition_up, condition_down)):
            @pl.when(condition)
            def _(side=side):
                act(side)

    at_sides(has_above, has_below, lambda side: greet((up, down)[side]))
    for peer in (sibling, partner, diagonal):
        greet({"rcv": peer})
    def halo_copy(side, piece):
        target, their = ((up, up_rcv), (down, down_rcv))[side]
        return pltpu.make_async_remote_copy(
            src_ref=u_hbm.at[pl.ds(first_of(their), quarter), :, :, :, pl.ds(pl.multiple_of(piece * LANES, LANES), LANES)],
            dst_ref=halo.at[side, piece], send_sem=halo_send.at[side], recv_sem=halo_recv.at[side, piece],
            device_id=target, device_id_type=MESH)

    def extra_copy(side, n):
        target, their = ((up, up_rcv), (down, down_rcv))[side]
        return pltpu.make_async_remote_copy(
            src_ref=u_hbm.at[pl.ds(others_of(their), EXTRA), :, :, :, pl.ds((pieces - 2 + n) * LANES, LANES)],
            dst_ref=extra.at[side, n], send_sem=extra_send.at[side], recv_sem=extra_recv.at[side, n],
            device_id=target, device_id_type=MESH)

    def to_sibling(step, whose):
        half_of = pl.ds((chip + whose - 2 * chip * whose) * quarter, quarter)
        return pltpu.make_async_remote_copy(
            src_ref=adj.at[step, 1 - core, :, half_of], dst_ref=from_sib.at[step, :, half_of],
            send_sem=sib_send, recv_sem=sib_recv.at[step, whose],
            device_id={"rcv": sibling}, device_id_type=MESH)

    def to_partner(step, skip):
        part = pl.ds(skip, quarter - skip)
        return pltpu.make_async_remote_copy(
            src_ref=to_par.at[step, :, part], dst_ref=from_par.at[step, :, part],
            send_sem=par_send.at[min(skip, 1)], recv_sem=par_recv.at[step],
            device_id={"rcv": partner}, device_id_type=MESH)

    def red_copy(which, piece):
        target = (sibling, partner, diagonal)[which]
        return pltpu.make_async_remote_copy(
            src_ref=kpart.at[piece, target], dst_ref=red.at[which, piece],
            send_sem=red_send, recv_sem=red_recv.at[which],
            device_id={"rcv": target}, device_id_type=MESH)

    a, b = iota2((slots, stations * snaps), 0), iota2((slots, stations * snaps), 1)
    lag = (a & (snaps - 1)) - (b & (snaps - 1)) + lags // 2
    taps = jnp.zeros((slots, stations * snaps), F32)
    for source in range(sources):
        for station in range(stations):
            used = pairs[source, station].astype(F32)
            here = ((a // snaps) == source) & ((b // snaps) == station)
            for j in range(lags):
                taps = taps + jnp.where(here & (lag == j), filt[source, station, j] * used, 0.0)
    high = taps.astype(BF16)
    low = (taps - high.astype(F32)).astype(BF16)
    size, depth = slots * HALF, stations * snaps * HALF
    spread = ((iota2((size, slots), 0) >> 3) == iota2((size, slots), 1)).astype(BF16)
    spread_t = (iota2((stations * snaps, depth), 0) == (iota2((stations * snaps, depth), 1) >> 3)).astype(BF16)
    same_row = ((iota2((size, depth), 0) ^ iota2((size, depth), 1)) & (HALF - 1)) == 0
    for n, part in enumerate((high, low)):
        tall = jnp.dot(spread, part, preferred_element_type=F32).astype(BF16)
        mixer[n * size:(n + 1) * size] = jnp.where(
            same_row, jnp.dot(tall, spread_t, preferred_element_type=F32), 0.0).astype(BF16)

    def send_halo(first, last):
        def send(side):
            for piece in range(first, last):
                halo_copy(side, piece).start()
            if last == pieces:
                for n in range(2):
                    extra_copy(side, n).start()

        at_sides(has_above, has_below, send)

    def blank(side):
        halo[side] = jnp.zeros(halo.shape[1:], BF16)
        extra[side] = jnp.zeros(extra.shape[1:], BF16)

    lam_copy.wait()
    mu_copy.wait()

    half = slots // 2

    def early(step):
        block, plane = step // 2, step % 2

        g_copy(step).wait()

        @pl.when(step == 0)
        def _():
            u_copy.start()

        @pl.when(step + 1 < steps)
        def _():
            g_copy(step + 1).start()

        def mix(c):
            g = gv[block, :, c, plane].astype(F32)
            for part in range(2):
                rows = g[:, part * HALF:(part + 1) * HALF].reshape(depth, WIDE).astype(BF16)
                both = jnp.dot(mixer[...], rows, preferred_element_type=F32)
                hbuf[c, part] = both[:size] + both[size:]

        for c in range(5):
            mix(c)
        start = pl.multiple_of(block * WIDE, WIDE)
        lam = lamv[plane, :, pl.ds(start, WIDE)]
        shear = 2.0 * muv[plane, :, pl.ds(start, WIDE)]

        def mixed(c, at):
            rows = pl.ds(pl.multiple_of(at * HALF, HALF), HALF)
            return jnp.concatenate([hbuf[c, 0, rows], hbuf[c, 1, rows]], axis=0)

        for source in range(sources):
            def turn(t, _):
                h = [mixed(c, source * snaps + t) for c in range(5)]
                adj[step, source, 0, t] = shear * h[4]
                adj[step, source, 1, t] = shear * h[3]
                adj[step, source, 2, t] = lam * (h[0] + h[1] + h[2]) + shear * h[2]
                return 0

            lax.fori_loop(0, snaps, turn, 0, unroll=4)

        @pl.when(step == 0)
        def _():
            pl.semaphore_wait(barrier, 3 + count_above + count_below)
            send_halo(0, min(FIRST, pieces))

        to_sibling(step, 1).start()
        to_sibling(step, 0).start()

        def share():
            to_sibling(step, 1).wait_recv()

            def pass_on(n, _):
                t = (1 - chip) * quarter + n
                for k in range(3):
                    to_par[step, k, n] = (adj[step, core, k, t] + from_sib[step, k, t]).astype(BF16)
                return 0

            lax.fori_loop(0, quarter, pass_on, 0, unroll=4)

            @pl.when(step < steps - 2)
            def _():
                to_partner(step, 0).start()

            @pl.when(step >= steps - 2)
            def _():
                to_partner(step, EXTRA).start()

        mix(5)

        @pl.when(step == 0)
        def _():
            send_halo(min(FIRST, pieces), pieces)
            at_sides(slab == 0, slab == slabs - 1, blank)
            i, o = iota2(colmat.shape, 0), iota2(colmat.shape, 1)
            colmat[...] = stencil(i - LANES - o).astype(BF16)
            i, o = iota2(rowmat.shape, 1), iota2(rowmat.shape, 0)
            rowmat[...] = jnp.where((i >> 4) == (o >> 4), stencil(i - o), 0.0).astype(BF16)
            edge = jnp.zeros(uv.shape[:-1] + (LANES,), BF16)
            share()
            u_copy.wait()
            uv[:, :, :, :, :LANES] = edge
            uv[:, :, :, :, LANES + cols:] = edge

        for k in range(3):
            around = uv[:, k, plane, :, pl.ds(start, 2 * WIDE)].reshape(slots * ROW, 2 * WIDE)
            dxb[k] = jnp.dot(around, colmat[...], preferred_element_type=F32)
            inside = pl.ds(pl.multiple_of(start + LANES, LANES), WIDE)
            for part in range(2):
                rows = uv[part * half:(part + 1) * half, k, plane, :, inside].reshape(half * ROW, WIDE)
                dyb[k, part * half * ROW:(part + 1) * half * ROW] = jnp.dot(
                    rowmat[...], rows, preferred_element_type=F32)

        @pl.when(step > 0)
        def _():
            share()

        for source in range(sources):
            def weigh(t, carry):
                trace, rest = carry
                at = source * snaps + t
                here = pl.ds(pl.multiple_of(at * ROW, ROW), ROW)
                h = [mixed(c, at) for c in range(6)]
                dx = [dxb[k, here] for k in range(3)]
                dy = [dyb[k, here] for k in range(3)]
                trace = trace + (dx[0] + dy[1]) * (h[0] + h[1] + h[2])
                rest = rest + (dx[0] * h[0] + dy[1] * h[1] + dy[2] * h[3] + dx[2] * h[4] + (dy[0] + dx[1]) * h[5])
                return trace, rest

            zero = jnp.zeros((ROW, WIDE), F32)
            trace, rest = lax.fori_loop(0, snaps, weigh, (zero, zero), unroll=2)
            value = lam * trace + shear * rest
            for side in range(2):
                kacc[2 * block + side, source, plane] = value[:, side * LANES:(side + 1) * LANES]

    def late(piece, last):
        block, side = piece // 2, piece % 2
        lanes = pl.ds(pl.multiple_of(side * LANES, LANES), LANES)
        here = pl.ds(pl.multiple_of(LANES + piece * LANES, LANES), LANES)

        def add(totals, at, t, near, n, handed):
            new = list(totals)
            for k in range(3):
                f0, f1 = (uv[at, k, plane, :, here].astype(F32) for plane in range(2))
                b0, b1 = (near(0)[n, k, plane].astype(F32) for plane in range(2))
                a0, a1 = (near(1)[n, k, plane].astype(F32) for plane in range(2))
                slopes = 8.0 * (f1 - b1) - (a0 - b0), 8.0 * (a0 - f0) - (a1 - b1)
                for plane in range(2):
                    step = 2 * block + plane
                    whole = adj[step, core, k, t, :, lanes] + from_sib[step, k, t, :, lanes]
                    if handed:
                        whole = whole + from_par[step, k, n, :, lanes].astype(F32)
                    new[plane] = new[plane] + slopes[plane] * whole
            return tuple(new)

        def mine(n, totals, handed=True):
            return add(totals, first_of(rcv) + n, chip * quarter + n, lambda s: halo.at[s, piece], n, handed)

        totals = tuple(kacc[piece, core, plane] for plane in range(2))
        if last:
            for n in range(EXTRA):
                totals = mine(n, totals, False)
                totals = add(totals, others_of(rcv) + n, (1 - chip) * quarter + n, lambda s: extra.at[s, side], n, False)
        totals = lax.fori_loop(EXTRA if last else 0, quarter, mine, totals, unroll=True if last else 2)
        for plane in range(2):
            kacc[piece, core, plane] = totals[plane]

    def hand_out(piece):
        for source in range(sources):
            for plane in range(2):
                value = kacc[piece, source, plane] * (1.0 / 12.0)
                for owner in range(4):
                    kpart[piece, owner, source, plane] = value[owner * (ROW // 4):(owner + 1) * (ROW // 4)]
        for which in range(3):
            red_copy(which, piece).start()

    def compute(step, _):
        early(step)
        return 0

    def wait_adjoint(block, skip):
        for plane in range(2):
            to_sibling(2 * block + plane, 0).wait_recv()
            to_partner(2 * block + plane, skip).wait_recv()

    def finish(piece, _):
        @pl.when(piece % 2 == 0)
        def _():
            wait_adjoint(piece // 2, 0)

        at_sides(has_below, has_above, lambda side: halo_copy(side, piece).wait_recv())
        late(piece, False)
        hand_out(piece)
        return 0

    lax.fori_loop(0, steps, compute, 0)
    lax.fori_loop(0, pieces - 2, finish, 0)
    wait_adjoint(blocks - 1, EXTRA)
    for n in range(2):
        def wait_halo(side):
            halo_copy(side, pieces - 2 + n).wait_recv()
            extra_copy(side, n).wait_recv()

        at_sides(has_below, has_above, wait_halo)
        late(pieces - 2 + n, True)
        hand_out(pieces - 2 + n)

    def all_sent(block, sem):
        pltpu.make_async_remote_copy(
            src_ref=block, dst_ref=block, send_sem=sem, recv_sem=sem,
            device_id={"rcv": sibling}, device_id_type=MESH).wait_send()

    at_sides(has_above, has_below, lambda side: all_sent(halo.at[side], halo_send.at[side]))
    all_sent(from_sib, sib_send)
    at_sides(has_above, has_below, lambda side: all_sent(extra.at[side], extra_send.at[side]))
    all_sent(from_par.at[pl.ds(0, steps - 2)], par_send.at[0])
    all_sent(from_par.at[pl.ds(steps - 2, 2), :, pl.ds(EXTRA, quarter - EXTRA)], par_send.at[1])
    all_sent(red, red_send)
    for which in range(3):
        pltpu.make_async_copy(red.at[which], red.at[which], red_recv.at[which]).wait()
    for piece in range(pieces):
        out_ref[:, :, :, piece * LANES:(piece + 1) * LANES] = (
            (kpart[piece, rcv] + red[0, piece]) + (red[1, piece] + red[2, piece]))


def on_device(displacement, green, lame_lambda, shear_modulus, filters, pairs):
    sources, snaps, parts, planes, rows, cols = displacement.shape
    stations, lags = filters.shape[1:]
    slots, taps = sources * snaps, stations * snaps
    pieces, blocks, quarter = cols // LANES, cols // WIDE, slots // 4
    size, depth, steps = slots * ROW, taps * ROW, blocks * planes
    anywhere = pl.BlockSpec(memory_space=pl.ANY)
    scalars = pl.BlockSpec(memory_space=pltpu.SMEM)
    dma = pltpu.SemaphoreType.DMA
    return pl.pallas_call(
        functools.partial(kernel, sources, snaps, stations, lags),
        out_shape=jax.ShapeDtypeStruct((sources, planes, rows // 4, cols), F32),
        in_specs=[anywhere] * 4 + [scalars] * 2,
        out_specs=pl.BlockSpec(memory_space=pltpu.VMEM),
        scratch_shapes=[
            pltpu.VMEM((slots, parts, planes, rows, cols + 2 * LANES), BF16),
            pltpu.VMEM((blocks, taps, 6, planes, rows, WIDE), BF16),
            pltpu.VMEM((planes, rows, cols), F32),
            pltpu.VMEM((planes, rows, cols), F32),
            pltpu.VMEM((2, pieces, quarter, parts, planes, rows, LANES), BF16),
            pltpu.VMEM((2, 2, EXTRA, parts, planes, rows, LANES), BF16),
            pltpu.VMEM((steps, sources, 3, snaps, rows, WIDE), F32),
            pltpu.VMEM((steps, 3, snaps, rows, WIDE), F32),
            pltpu.VMEM((steps, 3, quarter, rows, WIDE), BF16),
            pltpu.VMEM((steps, 3, quarter, rows, WIDE), BF16),
            pltpu.VMEM((6, 2, size // 2, WIDE), F32),
            pltpu.VMEM((3, size, WIDE), F32),
            pltpu.VMEM((3, size, WIDE), F32),
            pltpu.VMEM((size, depth // 2), BF16),
            pltpu.VMEM((2 * WIDE, WIDE), BF16),
            pltpu.VMEM((size // 2, size // 2), BF16),
            pltpu.VMEM((pieces, sources, planes, rows, LANES), F32),
            pltpu.VMEM((pieces, 4, sources, planes, rows // 4, LANES), F32),
            pltpu.VMEM((3, pieces, sources, planes, rows // 4, LANES), F32),
            dma, dma((steps,)), dma, dma,
            dma((2,)), dma((2, pieces)), dma((2,)), dma((2, 2)), dma, dma((steps, 2)), dma((2,)), dma((steps,)),
            dma, dma((3,)),
        ],
        compiler_params=pltpu.CompilerParams(
            collective_id=0, has_side_effects=True, vmem_limit_bytes=60 << 20),
        cost_estimate=pl.CostEstimate(flops=26_000_000_000, bytes_accessed=20_000_000, transcendentals=0),
    )(
        displacement.reshape(slots, parts, planes, rows, cols),
        green.reshape(taps, 6, planes, rows, cols),
        lame_lambda, shear_modulus, filters, pairs,
    )


def solution(mesh):
    placed = (
        P(None, None, None, "slab", None, None),
        P("rcv", None, None, "slab", None, None),
        P("slab", None, None),
        P("slab", None, None),
        P(None, "rcv", None),
        P(None, "rcv"),
    )
    return jax.shard_map(
        on_device,
        mesh=mesh,
        in_specs=placed,
        out_specs=P(None, "slab", "rcv", None),
        check_vma=False,
    )
```
